32 devices in a mesh: dp: 16 (over z, y, x), tensor: 2 (over core).
Axes of the slice: x: 2, y: 2, z: 4, core: 2. Of those that a mesh axis runs over, the one named last changes fastest.
Arguments:
- activations: bfloat16 [2048, 2048], P('dp', 'tensor'), may hold values from -12 to 12
- dgrad: bfloat16 [2048, 4864], P('dp', 'tensor'), may hold values from -24 to 24
- coding: int32 [16, 4], replicated, may hold values from 0 to 4, as said below
- alive: int32 [16], replicated, may hold values from 0 to 1, as said below
Outputs:
- weight_grad: float32 [2048, 4864], P('dp', 'tensor')
The draws below stay inside these ranges and needn't reach their ends.
Inputs may be any that keep to these rules, and one draw needn't show every extreme that they name: Each entry is 0, 1, 2 or 4; coding[i, 0] is never 0; in each row the zeros come after all nonzero entries; rows 0 to 3 have no zero. Workers 0 to 3 are alive.
All inputs are finite; a program needn't handle non-finite values.
Results may differ from the reference program's by a relative error of at most 0.0003.
Values may be sent and summed in bfloat16 or wider, within the bound.
A program may use at most 128 MiB of HBM per device.

```python
import math
import jax
import jax.numpy as jnp
from jax import lax

D = 2048
ROWS = 128
SLOTS = 4
FF = 4864
TOKENS = 2048
N_DP = 16


def draw_activations(key, part):
    first, second = jax.random.split(jax.random.fold_in(key, 11), 2)
    row_scale = 10.0 ** jax.random.uniform(second, (TOKENS, 1), jnp.float32, -0.5, 0.5)
    base = jnp.clip(jax.random.normal(first, (TOKENS, D), jnp.float32), -3.5, 3.5)
    return jnp.clip(base * row_scale, -12.0, 12.0).astype(jnp.bfloat16)


def draw_dgrad(key, part):
    first, second, third = jax.random.split(jax.random.fold_in(key, 23), 3)
    row_scale = 10.0 ** jax.random.uniform(second, (TOKENS, 1), jnp.float32, -0.5, 0.5)
    column = jnp.arange(FF, dtype=jnp.float32)[None, :]
    jitter = jnp.exp(jax.random.uniform(third, (1, FF), jnp.float32, -0.5, 0.5))
    column_scale = 4.0 ** (column / FF - 0.5) * jitter
    base = jnp.clip(jax.random.normal(first, (TOKENS, FF), jnp.float32), -3.5, 3.5)
    return jnp.clip(base * row_scale * column_scale, -24.0, 24.0).astype(jnp.bfloat16)


def draw_coding(key, part):
    first, second, third = jax.random.split(jax.random.fold_in(key, 37), 3)
    draws = jax.random.randint(first, (N_DP,), 0, 10)
    counts = 1 + (draws >= 6).astype(jnp.int32) + (draws >= 8).astype(jnp.int32) + (draws >= 9).astype(jnp.int32)
    busiest = jax.random.randint(second, (), 0, N_DP)
    worker = jnp.arange(N_DP)
    counts = jnp.where((worker == busiest) | (worker < SLOTS), SLOTS, jnp.minimum(counts, SLOTS))
    powers = jax.random.randint(third, (N_DP, SLOTS), 0, 3)
    values = jnp.left_shift(jnp.ones((N_DP, SLOTS), jnp.int32), powers)
    slot_index = jnp.arange(SLOTS)[None, :]
    return jnp.where(slot_index < counts[:, None], values, 0).astype(jnp.int32)


def draw_alive(key, part):
    draws = jax.random.randint(jax.random.fold_in(key, 53), (N_DP,), 0, 8)
    worker = jnp.arange(N_DP)
    return jnp.where((draws < 7) | (worker < SLOTS), 1, 0).astype(jnp.int32)


def setup_inputs(seed: int = 0) -> dict:
    arg_keys = jax.random.split(jax.random.key(seed), 5)
    return {
        "activations": draw_activations(jax.random.fold_in(arg_keys[4], 71), 0),
        "dgrad": draw_dgrad(jax.random.fold_in(arg_keys[4], 71), 0),
        "coding": draw_coding(jax.random.fold_in(arg_keys[4], 71), 0),
        "alive": draw_alive(jax.random.fold_in(arg_keys[4], 71), 0),
    }


def pair_products(acts, grads, offset):
    moved_acts = jnp.roll(acts, -offset, axis=0)
    moved_grads = jnp.roll(grads, -offset, axis=0)
    cross_acts = jnp.einsum('pad,pbd->pab', acts, moved_acts, precision=lax.Precision.HIGHEST)
    cross_grads = jnp.einsum('paf,pbf->pab', grads, moved_grads, precision=lax.Precision.HIGHEST)
    return lax.optimization_barrier(jnp.sum(cross_acts * cross_grads, axis=(1, 2)))

def coded_squares(pairs, coefs, slots):
    total = jnp.zeros((coefs.shape[0],), jnp.float32)
    for first in range(slots):
        for second in range(slots):
            lower = min(first, second)
            spread = abs(first - second)
            total = total + coefs[:, first] * coefs[:, second] * jnp.roll(pairs[:, spread], -lower)
    return total

def reference(activations, dgrad, coding, alive):
    workers = N_DP
    acts = activations.astype(jnp.float32).reshape(workers, ROWS, D)
    grads = dgrad.astype(jnp.float32).reshape(workers, ROWS, FF)
    pairs = jnp.stack([pair_products(acts, grads, offset) for offset in range(SLOTS)], axis=1)
    coefs = coding.astype(jnp.float32)
    squares = coded_squares(pairs, coefs, SLOTS)
    limit = 8.0 * math.sqrt(ROWS)
    factor = jnp.minimum(1.0, limit / jnp.sqrt(squares / (D * FF) + 1e-06))
    scaled = alive.astype(jnp.float32) * factor
    weights = jnp.zeros((workers,), jnp.float32)
    for offset in range(SLOTS):
        weights = weights + jnp.roll(scaled * coefs[:, offset], offset)
    weighted = (acts * weights[:, None, None]).reshape(workers * ROWS, D)
    total = jnp.dot(weighted.T, grads.reshape(workers * ROWS, FF), precision=lax.Precision.HIGHEST)
    return total / (limit * math.sqrt(workers))
```

```python
import functools
import math

import jax
import jax.numpy as jnp
from jax import lax
from jax.experimental import pallas as pl
from jax.experimental.pallas import tpu as pltpu
from jax.sharding import PartitionSpec as P

LANES = 128
PLANE = 4
VMEM_BUDGET = 48 * 1024 * 1024


def passed_along(value, axis, by):
    length = lax.axis_size(axis)
    return lax.ppermute(value, axis, [(i, (i + by) % length) for i in range(length)])


def local(activations, dgrad, coding, alive):
    workers = lax.axis_size("dp")
    position = lax.axis_index("dp")
    slots = coding.shape[1]
    rows = activations.shape[0]
    width = activations.shape[1] * lax.axis_size("tensor")
    hidden = dgrad.shape[1] * lax.axis_size("tensor")
    limit = 8.0 * math.sqrt(rows)
    overall = 1.0 / (limit * math.sqrt(workers))
    pieces = [(activations, dgrad)]
    for offset in range(1, slots):
        pieces.append(passed_along((activations, dgrad), "dp", -offset))
    coef_row = lax.dynamic_index_in_dim(coding, position, 0, keepdims=False)
    scaled_rows = jnp.concatenate(
        [pieces[offset][0] * coef_row[offset].astype(jnp.bfloat16) for offset in range(slots)],
        axis=0,
    )
    stacked_grads = jnp.concatenate([pieces[offset][1] for offset in range(slots)], axis=0)
    term = lax.dot_general(
        lax.all_gather(scaled_rows, "tensor", axis=1, tiled=True),
        stacked_grads,
        (((0,), (0,)), ((), ())),
        preferred_element_type=jnp.float32,
    )
    squares = lax.psum(jnp.sum(term * term), "tensor")
    factor = jnp.minimum(1.0, limit / jnp.sqrt(squares / (width * hidden) + 1e-06))
    present = lax.dynamic_index_in_dim(alive, position, 0, keepdims=False).astype(jnp.float32)
    return lax.psum_scatter(
        term * (present * factor * overall), "dp", scatter_dimension=0, tiled=True
    )


def kernel(
    planes, slots, limit, overall, entries,
    acts_ref, grads_ref, coding_ref, alive_ref, out_ref,
    gbuf, xplane, xcross, xall, apart, apeer, msend, mrecv, lhs,
    lsem, s_line, r_line, s_aline, r_aline, s_pair, r_pair, s_one, r_one,
    s_x, r_x, s_a2a, r_a2a, s_m, r_m,
):
    rows, half = acts_ref.shape
    cols = grads_ref.shape[1]
    n = planes * PLANE
    d = lax.axis_index("dp")
    t = lax.axis_index("tensor")
    z = d // PLANE
    c = lax.rem(d, PLANE)
    x = lax.rem(c, 2)
    y = c // 2
    cx = y * 2 + (1 - x)
    cy = (1 - y) * 2 + x
    xpeer = (z * PLANE + cx, t)
    ypeer = (z * PLANE + cy, t)
    other = (d, 1 - t)
    top = planes - 1

    def at_plane(plane):
        return (plane * PLANE + c, t)

    tiles = cols // LANES
    na = max(1, (tiles * 2 + 10) // 19)
    nb = (tiles - 2 * na + 1) // 2
    ga = (0, na * LANES)
    gd = (na * LANES, na * LANES)
    gad = (0, 2 * na * LANES)
    gb = (2 * na * LANES, nb * LANES)
    gc = ((2 * na + nb) * LANES, cols - (2 * na + nb) * LANES)
    gbc = (2 * na * LANES, cols - 2 * na * LANES)

    def g(slot, count, group):
        start = slot * rows
        return gbuf.at[pl.ds(pl.multiple_of(start, rows), rows * count), pl.ds(*group)]

    def remote(ref, dst, send, recv, peer):
        return pltpu.make_async_remote_copy(
            src_ref=ref, dst_ref=dst, send_sem=send, recv_sem=recv,
            device_id=peer, device_id_type=pl.DeviceIdType.MESH,
        )

    loads = [
        pltpu.make_async_copy(grads_ref, g(d, 1, (0, cols)), lsem.at[0]),
        pltpu.make_async_copy(
            acts_ref, xplane.at[pl.ds(pl.multiple_of(c * rows, rows), rows), :], lsem.at[1]
        ),
    ]
    for load in loads:
        load.start()
    barrier = pltpu.get_barrier_semaphore()

    def greet(peer):
        pl.semaphore_signal(barrier, inc=1, device_id=peer, device_id_type=pl.DeviceIdType.MESH)

    for peer in (xpeer, ypeer, other):
        greet(peer)
    for step in range(1, planes):
        greet(at_plane(lax.rem(z + step, planes)))
    pl.semaphore_wait(barrier, 2 + planes)
    for load in loads:
        load.wait()

    def line(plane, up):
        peer = at_plane(jnp.minimum(z + 1, top) if up else jnp.maximum(z - 1, 0))
        ref = g(plane * PLANE + c, 1, gbc)
        return remote(ref, ref, s_line.at[int(up), plane], r_line.at[plane], peer)

    def aline(plane, up):
        peer = at_plane(jnp.minimum(z + 1, top) if up else jnp.maximum(z - 1, 0))
        ref = g(plane * PLANE, PLANE, gad)
        return remote(ref, ref, s_aline.at[int(up), plane], r_aline.at[plane], peer)

    def pair(kind, plane):
        slot, group, peer = {
            0: (c, gb, ypeer),
            1: (c, gc, xpeer),
            2: (c, gb, xpeer),
            3: (cy, gb, xpeer),
            4: (c, gc, ypeer),
            5: (cx, gc, ypeer),
        }[kind]
        ref = g(plane * PLANE + slot, 1, group)
        return remote(ref, ref, s_pair.at[kind, plane], r_pair.at[kind, plane], peer)

    def one(kind):
        slot, count, group, peer = {
            0: (c, 1, ga, xpeer),
            1: (c, 1, gd, ypeer),
            2: (y * 2, 2, ga, ypeer),
            3: (c, 1, gd, xpeer),
            4: (cy, 1, gd, xpeer),
        }[kind]
        ref = g(z * PLANE + slot, count, group)
        return remote(ref, ref, s_one.at[kind], r_one.at[kind], peer)

    def xrows(slot, part=None):
        if part is None:
            return xplane.at[pl.ds(pl.multiple_of(slot * rows, rows), rows), :]
        size = rows // 2
        return xplane.at[pl.ds(pl.multiple_of(slot * rows + part * size, size), size), :]

    def xcopy(kind):
        ref, dst, peer = {
            0: (xrows(c), xrows(c), xpeer),
            1: (xrows(c), xrows(c), ypeer),
            2: (xrows(cx, 0), xrows(cx, 0), ypeer),
            3: (xrows(cy, 1), xrows(cy, 1), xpeer),
            4: (xrows(c), xcross, at_plane(lax.rem(z + top, planes))),
        }[kind]
        return remote(ref, dst, s_x.at[kind], r_x.at[kind], peer)

    def in_line(plane, sign, action):
        ok = (plane >= 0) if sign < 0 else (plane <= top)

        @pl.when(ok)
        def _():
            action(plane)

    def both(step, action):
        in_line(z - 1 - step, -1, functools.partial(action, up=True))
        in_line(z + 1 + step, 1, functools.partial(action, up=False))

    def forward(make, plane, up):
        @pl.when((z < top) if up else (z > 0))
        def _():
            make(plane, up).start()

    def start_pairs(kinds, plane):
        for kind in kinds:
            pair(kind, plane).start()

    one(0).start()
    one(1).start()
    for up in (True, False):
        forward(line, z, up)
    pair(1, z).start()
    pair(0, z).start()
    one(0).wait_recv()
    one(2).start()
    one(1).wait_recv()
    one(3).start()
    one(4).start()
    xcopy(0).start()
    xcopy(1).start()
    start_pairs((2, 4), z)
    for kind in (2, 3, 4):
        one(kind).wait_recv()
    for up in (True, False):
        forward(aline, z, up)
    xcopy(4).start()
    pair(1, z).wait_recv()
    pair(5, z).start()
    pair(0, z).wait_recv()
    pair(3, z).start()

    def line_arrived(plane, up):
        line(plane, up).wait_recv()
        forward(line, plane, up)
        start_pairs((0, 1, 2, 4), plane)

    def aline_arrived(plane, up):
        aline(plane, up).wait_recv()
        forward(aline, plane, up)

    def second(plane, up):
        pair(1, plane).wait_recv()
        pair(5, plane).start()
        pair(0, plane).wait_recv()
        pair(3, plane).start()

    both(0, line_arrived)
    xcopy(0).wait_recv()
    xcopy(2).start()
    xcopy(1).wait_recv()
    xcopy(3).start()
    both(0, aline_arrived)
    xcopy(2).wait_recv()
    xcopy(3).wait_recv()

    feats = xall.shape[1]
    per = half // (PLANE * feats)
    holder = z // per

    def share(plane):
        offset = (plane - t * per) * PLANE * feats + c * feats
        src = xplane.at[:, pl.ds(pl.multiple_of(offset, feats), feats)]
        dst = xall.at[pl.ds(pl.multiple_of(z * PLANE * rows, rows), PLANE * rows), :]
        return src, dst

    def a2a(plane, source):
        src, dst = share(plane)
        return remote(src, dst, s_a2a.at[plane], r_a2a.at[source], at_plane(plane))

    def local_share():
        src, dst = share(z)
        return pltpu.make_async_copy(src, dst, lsem.at[2])

    for plane in range(planes):
        @pl.when((plane // per == t) & (plane != z))
        def _(plane=plane):
            a2a(plane, z).start()

    @pl.when(holder == t)
    def _():
        local_share().start()

    xcopy(4).wait_recv()
    dims = (((1,), (1,)), ((), ()))
    own_x = xplane[pl.ds(pl.multiple_of(c * rows, rows), rows), :]
    apart[:rows, :] = lax.dot_general(own_x, xplane[...], dims, preferred_element_type=jnp.float32)
    apart[rows:, :] = lax.dot_general(
        xcross[...], xplane[...], dims, preferred_element_type=jnp.float32
    )

    both(0, second)
    both(1, line_arrived)
    both(1, aline_arrived)
    exchange = remote(apart, apeer, s_one.at[5], r_one.at[5], other)
    exchange.start()
    both(2, line_arrived)
    both(1, second)

    whole = remote(xall, xall, s_one.at[6], r_one.at[6], other)

    @pl.when(holder == t)
    def _():
        for step in range(1, planes):
            a2a(z, lax.rem(z + step, planes)).wait_recv()
        local_share().wait()
        whole.start()

    @pl.when(holder != t)
    def _():
        whole.wait_recv()

    both(2, second)

    exchange.wait()
    apart[...] = apart[...] + apeer[...]
    row = lax.broadcasted_iota(jnp.int32, (n, LANES), 0)
    lane = lax.broadcasted_iota(jnp.int32, (n, LANES), 1)
    coefs = jnp.zeros((n, LANES), jnp.float32)
    for slot in range(slots):
        coefs = coefs + jnp.where(
            lane == lax.rem(row + slot, n), coding_ref[:, slot : slot + 1].astype(jnp.float32), 0.0
        )

    both(2, aline_arrived)
    for plane in range(planes):
        for kind in (2, 3, 4, 5):
            pair(kind, plane).wait_recv()

    def products(slot, base):
        block = gbuf[pl.ds(pl.multiple_of(slot * rows, rows), rows), :]
        plane_rows = gbuf[pl.ds(pl.multiple_of(z * PLANE * rows, rows), PLANE * rows), :]
        grams = lax.dot_general(block, plane_rows, dims, preferred_element_type=jnp.float32)
        sums = jnp.sum(grams * apart[base : base + rows, :], axis=0, keepdims=True)
        return [
            jnp.sum(sums[:, k * rows : (k + 1) * rows], axis=1, keepdims=True) for k in range(PLANE)
        ]

    ahead = lax.rem(z + 1, planes) * PLANE + c
    total = jnp.zeros((n, LANES), jnp.float32)
    for k, value in enumerate(products(d, 0)):
        total = total + jnp.where((row == z * PLANE + k) & (lane == d), value, 0.0)
    for k, value in enumerate(products(ahead, rows)):
        p = z * PLANE + k
        here = ((row == p) & (lane == ahead)) | ((row == ahead) & (lane == p))
        total = total + jnp.where(here, value, 0.0)
    for index, peer in enumerate((other, xpeer, ypeer)):
        msend[index] = total
        hop = remote(msend.at[index], mrecv.at[index], s_m.at[index], r_m.at[index], peer)
        hop.start()
        hop.wait()
        total = total + mrecv[index]
    msend[3] = total
    hops = []
    for step in range(1, planes):
        hops.append(
            remote(
                msend.at[3], mrecv.at[2 + step], s_m.at[2 + step], r_m.at[2 + step],
                at_plane(lax.rem(z + step, planes)),
            )
        )
        hops[-1].start()
    for hop in hops:
        hop.wait()
    for step in range(1, planes):
        total = total + mrecv[2 + step]

    spread = jnp.zeros((n, LANES), jnp.float32)
    for p in range(n):
        spread = spread + coefs[:, p : p + 1] * total[p : p + 1, :]
    squares = jnp.sum(spread * coefs, axis=1, keepdims=True)
    factor = jnp.minimum(1.0, limit / jnp.sqrt(squares / entries + 1e-06))
    scaled = alive_ref[...].astype(jnp.float32) * factor * overall
    weights = jnp.sum(scaled * coefs, axis=0, keepdims=True)

    for p in range(n):
        block = jnp.transpose(xall[p * rows : (p + 1) * rows, :].astype(jnp.float32))
        block = block * weights[:, p : p + 1]
        high = block.astype(jnp.bfloat16)
        lhs[:feats, p * rows : (p + 1) * rows] = high
        lhs[feats:, p * rows : (p + 1) * rows] = (block - high.astype(jnp.float32)).astype(
            jnp.bfloat16
        )

    def write(start, size):
        both_parts = jnp.dot(
            lhs[...], gbuf[:, pl.ds(start, size)], preferred_element_type=jnp.float32
        )
        out_ref[:, pl.ds(start, size)] = both_parts[:feats] + both_parts[feats:]

    wide = 2 * LANES

    @pl.loop(0, cols // wide)
    def _(tile):
        write(pl.multiple_of(tile * wide, wide), wide)

    if cols % wide:
        write(cols - cols % wide, cols % wide)

    for kind in range(5):
        one(kind).wait_send()
        xcopy(kind).wait_send()
    for plane in range(planes):
        for kind in range(6):
            pair(kind, plane).wait_send()

        @pl.when((plane // per == t) & (plane != z))
        def _(plane=plane):
            a2a(plane, z).wait_send()

        @pl.when((plane <= z) & (z < top))
        def _(plane=plane):
            line(plane, True).wait_send()
            aline(plane, True).wait_send()

        @pl.when((plane >= z) & (z > 0))
        def _(plane=plane):
            line(plane, False).wait_send()
            aline(plane, False).wait_send()

    @pl.when(holder == t)
    def _():
        whole.wait_send()


def gathered(activations, dgrad, coding, alive):
    workers = lax.axis_size("dp")
    rows, half = activations.shape
    cols = dgrad.shape[1]
    tensor = lax.axis_size("tensor")
    planes = workers // PLANE
    feats = half * tensor // workers
    limit = 8.0 * math.sqrt(rows)
    overall = 1.0 / (limit * math.sqrt(workers))
    body = functools.partial(
        kernel, planes, coding.shape[1], limit, overall, float(half * tensor * cols * tensor)
    )
    dma = pltpu.SemaphoreType.DMA
    vmem = pl.BlockSpec(memory_space=pltpu.VMEM)
    return pl.pallas_call(
        body,
        out_shape=jax.ShapeDtypeStruct((feats, cols), jnp.float32),
        in_specs=[pl.BlockSpec(memory_space=pl.ANY)] * 2 + [vmem] * 2,
        out_specs=vmem,
        scratch_shapes=[
            pltpu.VMEM((workers * rows, cols), jnp.bfloat16),
            pltpu.VMEM((PLANE * rows, half), jnp.bfloat16),
            pltpu.VMEM((rows, half), jnp.bfloat16),
            pltpu.VMEM((workers * rows, feats), jnp.bfloat16),
            pltpu.VMEM((2 * rows, PLANE * rows), jnp.float32),
            pltpu.VMEM((2 * rows, PLANE * rows), jnp.float32),
            pltpu.VMEM((4, workers, LANES), jnp.float32),
            pltpu.VMEM((2 + planes, workers, LANES), jnp.float32),
            pltpu.VMEM((2 * feats, workers * rows), jnp.bfloat16),
            dma((3,)),
            dma((2, planes)),
            dma((planes,)),
            dma((2, planes)),
            dma((planes,)),
            dma((6, planes)),
            dma((6, planes)),
            dma((7,)),
            dma((7,)),
            dma((5,)),
            dma((5,)),
            dma((planes,)),
            dma((planes,)),
            dma((2 + planes,)),
            dma((2 + planes,)),
        ],
        compiler_params=pltpu.CompilerParams(
            collective_id=0, has_side_effects=True, vmem_limit_bytes=VMEM_BUDGET
        ),
    )(activations, dgrad, coding, alive.reshape(workers, 1))


def fits(activations, dgrad, coding):
    workers = lax.axis_size("dp")
    rows, half = activations.shape
    cols = dgrad.shape[1]
    tensor = lax.axis_size("tensor")
    width = half * tensor
    planes = workers // PLANE
    return (
        tensor == 2
        and workers % PLANE == 0
        and PLANE <= workers <= LANES
        and planes >= 3
        and planes % tensor == 0
        and coding.shape[1] <= PLANE
        and rows == LANES
        and width == workers * LANES
        and cols % LANES == 0
        and cols >= 8 * LANES
        and workers * rows * cols * 2 <= VMEM_BUDGET // 2
    )


def step(activations, dgrad, coding, alive):
    if fits(activations, dgrad, coding):
        return gathered(activations, dgrad, coding, alive)
    return local(activations, dgrad, coding, alive)


def solution(mesh):
    return jax.shard_map(
        step,
        mesh=mesh,
        in_specs=(P("dp", "tensor"), P("dp", "tensor"), P(), P()),
        out_specs=P("dp", "tensor"),
        check_vma=False,
    )
```

```python
import functools
import math

import jax
import jax.numpy as jnp
from jax import lax
from jax.experimental import pallas as pl
from jax.experimental.pallas import tpu as pltpu
from jax.sharding import PartitionSpec as P

LANES = 128
PLANE = 4
VMEM_BUDGET = 48 * 1024 * 1024


def passed_along(value, axis, by):
    length = lax.axis_size(axis)
    return lax.ppermute(value, axis, [(i, (i + by) % length) for i in range(length)])


def local(activations, dgrad, coding, alive):
    workers = lax.axis_size("dp")
    position = lax.axis_index("dp")
    slots = coding.shape[1]
    rows = activations.shape[0]
    width = activations.shape[1] * lax.axis_size("tensor")
    hidden = dgrad.shape[1] * lax.axis_size("tensor")
    limit = 8.0 * math.sqrt(rows)
    overall = 1.0 / (limit * math.sqrt(workers))
    pieces = [(activations, dgrad)]
    for offset in range(1, slots):
        pieces.append(passed_along((activations, dgrad), "dp", -offset))
    coef_row = lax.dynamic_index_in_dim(coding, position, 0, keepdims=False)
    scaled_rows = jnp.concatenate(
        [pieces[offset][0] * coef_row[offset].astype(jnp.bfloat16) for offset in range(slots)],
        axis=0,
    )
    stacked_grads = jnp.concatenate([pieces[offset][1] for offset in range(slots)], axis=0)
    term = lax.dot_general(
        lax.all_gather(scaled_rows, "tensor", axis=1, tiled=True),
        stacked_grads,
        (((0,), (0,)), ((), ())),
        preferred_element_type=jnp.float32,
    )
    squares = lax.psum(jnp.sum(term * term), "tensor")
    factor = jnp.minimum(1.0, limit / jnp.sqrt(squares / (width * hidden) + 1e-06))
    present = lax.dynamic_index_in_dim(alive, position, 0, keepdims=False).astype(jnp.float32)
    return lax.psum_scatter(
        term * (present * factor * overall), "dp", scatter_dimension=0, tiled=True
    )


def kernel(
    planes, slots, limit, overall, entries,
    acts_ref, grads_ref, coding_ref, alive_ref, out_ref,
    gbuf, xplane, xcross, xall, apart, apeer, msend, mrecv, lhs,
    lsem, s_line, r_line, s_aline, r_aline, s_pair, r_pair, s_one, r_one,
    s_x, r_x, s_a2a, r_a2a, s_m, r_m,
):
    rows, half = acts_ref.shape
    cols = grads_ref.shape[1]
    n = planes * PLANE
    d = lax.axis_index("dp")
    t = lax.axis_index("tensor")
    z = d // PLANE
    c = lax.rem(d, PLANE)
    x = lax.rem(c, 2)
    y = c // 2
    cx = y * 2 + (1 - x)
    cy = (1 - y) * 2 + x
    xpeer = (z * PLANE + cx, t)
    ypeer = (z * PLANE + cy, t)
    diagonal = (z * PLANE + PLANE - 1 - c, t)
    other = (d, 1 - t)
    top = planes - 1

    def at_plane(plane):
        return (plane * PLANE + c, t)

    tiles = cols // LANES
    na = max(1, (tiles * 2 + 10) // 19)
    nb = (tiles - 2 * na + 1) // 2
    ga = (0, na * LANES)
    gd = (na * LANES, na * LANES)
    gad = (0, 2 * na * LANES)
    gb = (2 * na * LANES, nb * LANES)
    gc = ((2 * na + nb) * LANES, cols - (2 * na + nb) * LANES)
    gbc = (2 * na * LANES, cols - 2 * na * LANES)

    def g(slot, count, group):
        start = slot * rows
        return gbuf.at[pl.ds(pl.multiple_of(start, rows), rows * count), pl.ds(*group)]

    def remote(ref, dst, send, recv, peer):
        return pltpu.make_async_remote_copy(
            src_ref=ref, dst_ref=dst, send_sem=send, recv_sem=recv,
            device_id=peer, device_id_type=pl.DeviceIdType.MESH,
        )

    loads = [
        pltpu.make_async_copy(grads_ref, g(d, 1, (0, cols)), lsem.at[0]),
        pltpu.make_async_copy(
            acts_ref, xplane.at[pl.ds(pl.multiple_of(c * rows, rows), rows), :], lsem.at[1]
        ),
    ]
    for load in loads:
        load.start()
    barrier = pltpu.get_barrier_semaphore()

    def greet(peer):
        pl.semaphore_signal(barrier, inc=1, device_id=peer, device_id_type=pl.DeviceIdType.MESH)

    others = [at_plane(lax.rem(z + step, planes)) for step in range(1, planes)]
    for peer in (xpeer, ypeer, diagonal, other, *others):
        greet(peer)
    pl.semaphore_wait(barrier, 3 + planes)
    for load in loads:
        load.wait()

    def line(plane, up):
        peer = at_plane(jnp.minimum(z + 1, top) if up else jnp.maximum(z - 1, 0))
        ref = g(plane * PLANE + c, 1, gbc)
        return remote(ref, ref, s_line.at[int(up), plane], r_line.at[plane], peer)

    def aline(plane, up):
        peer = at_plane(jnp.minimum(z + 1, top) if up else jnp.maximum(z - 1, 0))
        ref = g(plane * PLANE, PLANE, gad)
        return remote(ref, ref, s_aline.at[int(up), plane], r_aline.at[plane], peer)

    def pair(kind, plane):
        slot, group, peer = {
            0: (c, gb, ypeer),
            1: (c, gc, xpeer),
            2: (c, gb, xpeer),
            3: (cy, gb, xpeer),
            4: (c, gc, ypeer),
            5: (cx, gc, ypeer),
        }[kind]
        ref = g(plane * PLANE + slot, 1, group)
        return remote(ref, ref, s_pair.at[kind, plane], r_pair.at[kind, plane], peer)

    def one(kind):
        slot, count, group, peer = {
            0: (c, 1, ga, xpeer),
            1: (c, 1, gd, ypeer),
            2: (y * 2, 2, ga, ypeer),
            3: (c, 1, gd, xpeer),
            4: (cy, 1, gd, xpeer),
        }[kind]
        ref = g(z * PLANE + slot, count, group)
        return remote(ref, ref, s_one.at[kind], r_one.at[kind], peer)

    def xrows(slot, part=None):
        if part is None:
            return xplane.at[pl.ds(pl.multiple_of(slot * rows, rows), rows), :]
        size = rows // 2
        return xplane.at[pl.ds(pl.multiple_of(slot * rows + part * size, size), size), :]

    def xcopy(kind):
        ref, dst, peer = {
            0: (xrows(c), xrows(c), xpeer),
            1: (xrows(c), xrows(c), ypeer),
            2: (xrows(cx, 0), xrows(cx, 0), ypeer),
            3: (xrows(cy, 1), xrows(cy, 1), xpeer),
            4: (xrows(c), xcross, at_plane(lax.rem(z + top, planes))),
        }[kind]
        return remote(ref, dst, s_x.at[kind], r_x.at[kind], peer)

    def in_line(plane, sign, action):
        ok = (plane >= 0) if sign < 0 else (plane <= top)

        @pl.when(ok)
        def _():
            action(plane)

    def both(step, action):
        in_line(z - 1 - step, -1, functools.partial(action, up=True))
        in_line(z + 1 + step, 1, functools.partial(action, up=False))

    def forward(make, plane, up):
        @pl.when((z < top) if up else (z > 0))
        def _():
            make(plane, up).start()

    def start_pairs(kinds, plane):
        for kind in kinds:
            pair(kind, plane).start()

    one(0).start()
    one(1).start()
    for up in (True, False):
        forward(line, z, up)
    pair(1, z).start()
    pair(0, z).start()
    one(0).wait_recv()
    one(2).start()
    one(1).wait_recv()
    one(3).start()
    one(4).start()
    xcopy(0).start()
    xcopy(1).start()
    start_pairs((2, 4), z)
    for kind in (2, 3, 4):
        one(kind).wait_recv()
    for up in (True, False):
        forward(aline, z, up)
    xcopy(4).start()
    pair(1, z).wait_recv()
    pair(5, z).start()
    pair(0, z).wait_recv()
    pair(3, z).start()

    def line_arrived(plane, up):
        line(plane, up).wait_recv()
        forward(line, plane, up)
        start_pairs((0, 1, 2, 4), plane)

    def aline_arrived(plane, up):
        aline(plane, up).wait_recv()
        forward(aline, plane, up)

    def second(plane, up):
        pair(1, plane).wait_recv()
        pair(5, plane).start()
        pair(0, plane).wait_recv()
        pair(3, plane).start()

    both(0, line_arrived)
    xcopy(0).wait_recv()
    xcopy(2).start()
    xcopy(1).wait_recv()
    xcopy(3).start()
    both(0, aline_arrived)
    xcopy(2).wait_recv()
    xcopy(3).wait_recv()

    feats = xall.shape[1]
    per = half // (PLANE * feats)
    holder = z // per

    def share(plane):
        offset = (plane - t * per) * PLANE * feats + c * feats
        src = xplane.at[:, pl.ds(pl.multiple_of(offset, feats), feats)]
        dst = xall.at[pl.ds(pl.multiple_of(z * PLANE * rows, rows), PLANE * rows), :]
        return src, dst

    def a2a(plane, source):
        src, dst = share(plane)
        return remote(src, dst, s_a2a.at[plane], r_a2a.at[source], at_plane(plane))

    def local_share():
        src, dst = share(z)
        return pltpu.make_async_copy(src, dst, lsem.at[2])

    xcopy(4).wait_recv()
    dims = (((1,), (1,)), ((), ()))
    own_x = xplane[pl.ds(pl.multiple_of(c * rows, rows), rows), :]
    apart[:rows, :] = lax.dot_general(own_x, xplane[...], dims, preferred_element_type=jnp.float32)
    apart[rows:, :] = lax.dot_general(
        xcross[...], xplane[...], dims, preferred_element_type=jnp.float32
    )

    both(0, second)
    both(1, line_arrived)
    for plane in range(planes):
        @pl.when((plane // per == t) & (plane != z))
        def _(plane=plane):
            a2a(plane, z).start()

    @pl.when(holder == t)
    def _():
        local_share().start()

    both(1, aline_arrived)
    exchange = remote(apart, apeer, s_one.at[5], r_one.at[5], other)
    exchange.start()
    both(1, second)
    both(2, line_arrived)

    whole = remote(xall, xall, s_one.at[6], r_one.at[6], other)

    @pl.when(holder == t)
    def _():
        for step in range(1, planes):
            a2a(z, lax.rem(z + step, planes)).wait_recv()
        local_share().wait()
        whole.start()

    @pl.when(holder != t)
    def _():
        whole.wait_recv()

    both(2, second)

    exchange.wait()
    apart[...] = apart[...] + apeer[...]
    row = lax.broadcasted_iota(jnp.int32, (n, LANES), 0)
    lane = lax.broadcasted_iota(jnp.int32, (n, LANES), 1)
    coefs = jnp.zeros((n, LANES), jnp.float32)
    for slot in range(slots):
        coefs = coefs + jnp.where(
            lane == lax.rem(row + slot, n), coding_ref[:, slot : slot + 1].astype(jnp.float32), 0.0
        )

    both(2, aline_arrived)
    for plane in range(planes):
        for kind in (2, 3, 4, 5):
            pair(kind, plane).wait_recv()

    def products(slot, base):
        block = gbuf[pl.ds(pl.multiple_of(slot * rows, rows), rows), :]
        plane_rows = gbuf[pl.ds(pl.multiple_of(z * PLANE * rows, rows), PLANE * rows), :]
        grams = lax.dot_general(block, plane_rows, dims, preferred_element_type=jnp.float32)
        sums = jnp.sum(grams * apart[base : base + rows, :], axis=0, keepdims=True)
        return [
            jnp.sum(sums[:, k * rows : (k + 1) * rows], axis=1, keepdims=True) for k in range(PLANE)
        ]

    ahead = lax.rem(z + 1, planes) * PLANE + c
    total = jnp.zeros((n, LANES), jnp.float32)
    for k, value in enumerate(products(d, 0)):
        total = total + jnp.where((row == z * PLANE + k) & (lane == d), value, 0.0)
    for k, value in enumerate(products(ahead, rows)):
        p = z * PLANE + k
        here = ((row == p) & (lane == ahead)) | ((row == ahead) & (lane == p))
        total = total + jnp.where(here, value, 0.0)
    stages = ((other,), (diagonal, xpeer, ypeer), tuple(others))
    first = 0
    for stage, peers in enumerate(stages):
        msend[stage] = total
        hops = [
            remote(msend.at[stage], mrecv.at[first + k], s_m.at[first + k], r_m.at[first + k], peer)
            for k, peer in enumerate(peers)
        ]
        for hop in hops:
            hop.start()
        for hop in hops:
            hop.wait()
        for k in range(len(peers)):
            total = total + mrecv[first + k]
        first += len(peers)

    spread = jnp.zeros((n, LANES), jnp.float32)
    for p in range(n):
        spread = spread + coefs[:, p : p + 1] * total[p : p + 1, :]
    squares = jnp.sum(spread * coefs, axis=1, keepdims=True)
    factor = jnp.minimum(1.0, limit / jnp.sqrt(squares / entries + 1e-06))
    scaled = alive_ref[...].astype(jnp.float32) * factor * overall
    weights = jnp.sum(scaled * coefs, axis=0, keepdims=True)

    for p in range(n):
        block = jnp.transpose(xall[p * rows : (p + 1) * rows, :].astype(jnp.float32))
        block = block * weights[:, p : p + 1]
        high = block.astype(jnp.bfloat16)
        lhs[:feats, p * rows : (p + 1) * rows] = high
        lhs[feats:, p * rows : (p + 1) * rows] = (block - high.astype(jnp.float32)).astype(
            jnp.bfloat16
        )

    def write(start, size):
        both_parts = jnp.dot(
            lhs[...], gbuf[:, pl.ds(start, size)], preferred_element_type=jnp.float32
        )
        out_ref[:, pl.ds(start, size)] = both_parts[:feats] + both_parts[feats:]

    wide = 2 * LANES

    @pl.loop(0, cols // wide)
    def _(tile):
        write(pl.multiple_of(tile * wide, wide), wide)

    if cols % wide:
        write(cols - cols % wide, cols % wide)

    for kind in range(5):
        one(kind).wait_send()
        xcopy(kind).wait_send()
    for plane in range(planes):
        for kind in range(6):
            pair(kind, plane).wait_send()

        @pl.when((plane // per == t) & (plane != z))
        def _(plane=plane):
            a2a(plane, z).wait_send()

        @pl.when((plane <= z) & (z < top))
        def _(plane=plane):
            line(plane, True).wait_send()
            aline(plane, True).wait_send()

        @pl.when((plane >= z) & (z > 0))
        def _(plane=plane):
            line(plane, False).wait_send()
            aline(plane, False).wait_send()

    @pl.when(holder == t)
    def _():
        whole.wait_send()


def gathered(activations, dgrad, coding, alive):
    workers = lax.axis_size("dp")
    rows, half = activations.shape
    cols = dgrad.shape[1]
    tensor = lax.axis_size("tensor")
    planes = workers // PLANE
    feats = half * tensor // workers
    limit = 8.0 * math.sqrt(rows)
    overall = 1.0 / (limit * math.sqrt(workers))
    body = functools.partial(
        kernel, planes, coding.shape[1], limit, overall, float(half * tensor * cols * tensor)
    )
    dma = pltpu.SemaphoreType.DMA
    vmem = pl.BlockSpec(memory_space=pltpu.VMEM)
    return pl.pallas_call(
        body,
        out_shape=jax.ShapeDtypeStruct((feats, cols), jnp.float32),
        in_specs=[pl.BlockSpec(memory_space=pl.ANY)] * 2 + [vmem] * 2,
        out_specs=vmem,
        scratch_shapes=[
            pltpu.VMEM((workers * rows, cols), jnp.bfloat16),
            pltpu.VMEM((PLANE * rows, half), jnp.bfloat16),
            pltpu.VMEM((rows, half), jnp.bfloat16),
            pltpu.VMEM((workers * rows, feats), jnp.bfloat16),
            pltpu.VMEM((2 * rows, PLANE * rows), jnp.float32),
            pltpu.VMEM((2 * rows, PLANE * rows), jnp.float32),
            pltpu.VMEM((3, workers, LANES), jnp.float32),
            pltpu.VMEM((3 + planes, workers, LANES), jnp.float32),
            pltpu.VMEM((2 * feats, workers * rows), jnp.bfloat16),
            dma((3,)),
            dma((2, planes)),
            dma((planes,)),
            dma((2, planes)),
            dma((planes,)),
            dma((6, planes)),
            dma((6, planes)),
            dma((7,)),
            dma((7,)),
            dma((5,)),
            dma((5,)),
            dma((planes,)),
            dma((planes,)),
            dma((3 + planes,)),
            dma((3 + planes,)),
        ],
        compiler_params=pltpu.CompilerParams(
            collective_id=0, has_side_effects=True, vmem_limit_bytes=VMEM_BUDGET
        ),
    )(activations, dgrad, coding, alive.reshape(workers, 1))


def fits(activations, dgrad, coding):
    workers = lax.axis_size("dp")
    rows, half = activations.shape
    cols = dgrad.shape[1]
    tensor = lax.axis_size("tensor")
    width = half * tensor
    planes = workers // PLANE
    return (
        tensor == 2
        and workers % PLANE == 0
        and PLANE <= workers <= LANES
        and planes >= 3
        and planes % tensor == 0
        and coding.shape[1] <= PLANE
        and rows == LANES
        and width == workers * LANES
        and cols % LANES == 0
        and cols >= 8 * LANES
        and workers * rows * cols * 2 <= VMEM_BUDGET // 2
    )


def step(activations, dgrad, coding, alive):
    if fits(activations, dgrad, coding):
        return gathered(activations, dgrad, coding, alive)
    return local(activations, dgrad, coding, alive)


def solution(mesh):
    return jax.shard_map(
        step,
        mesh=mesh,
        in_specs=(P("dp", "tensor"), P("dp", "tensor"), P(), P()),
        out_specs=P("dp", "tensor"),
        check_vma=False,
    )
```

```python
import functools
import math

import jax
import jax.numpy as jnp
from jax import lax
from jax.experimental import pallas as pl
from jax.experimental.pallas import tpu as pltpu
from jax.sharding import PartitionSpec as P

LANES = 128
PLANE = 4
VMEM_BUDGET = 48 * 1024 * 1024


def passed_along(value, axis, by):
    length = lax.axis_size(axis)
    return lax.ppermute(value, axis, [(i, (i + by) % length) for i in range(length)])


def local(activations, dgrad, coding, alive):
    workers = lax.axis_size("dp")
    position = lax.axis_index("dp")
    slots = coding.shape[1]
    rows = activations.shape[0]
    width = activations.shape[1] * lax.axis_size("tensor")
    hidden = dgrad.shape[1] * lax.axis_size("tensor")
    limit = 8.0 * math.sqrt(rows)
    overall = 1.0 / (limit * math.sqrt(workers))
    pieces = [(activations, dgrad)]
    for offset in range(1, slots):
        pieces.append(passed_along((activations, dgrad), "dp", -offset))
    coef_row = lax.dynamic_index_in_dim(coding, position, 0, keepdims=False)
    scaled_rows = jnp.concatenate(
        [pieces[offset][0] * coef_row[offset].astype(jnp.bfloat16) for offset in range(slots)],
        axis=0,
    )
    stacked_grads = jnp.concatenate([pieces[offset][1] for offset in range(slots)], axis=0)
    term = lax.dot_general(
        lax.all_gather(scaled_rows, "tensor", axis=1, tiled=True),
        stacked_grads,
        (((0,), (0,)), ((), ())),
        preferred_element_type=jnp.float32,
    )
    squares = lax.psum(jnp.sum(term * term), "tensor")
    factor = jnp.minimum(1.0, limit / jnp.sqrt(squares / (width * hidden) + 1e-06))
    present = lax.dynamic_index_in_dim(alive, position, 0, keepdims=False).astype(jnp.float32)
    return lax.psum_scatter(
        term * (present * factor * overall), "dp", scatter_dimension=0, tiled=True
    )


def kernel(
    planes, slots, limit, overall, entries,
    acts_ref, grads_ref, coding_ref, alive_ref, out_ref,
    gbuf, xplane, xcross, xall, apart, apeer, msend, mrecv, lhs,
    lsem, s_line, r_line, s_aline, r_aline, s_pair, r_pair, s_one, r_one,
    s_x, r_x, s_a2a, r_a2a, s_m, r_m,
):
    rows, half = acts_ref.shape
    cols = grads_ref.shape[1]
    n = planes * PLANE
    d = lax.axis_index("dp")
    t = lax.axis_index("tensor")
    z = d // PLANE
    c = lax.rem(d, PLANE)
    x = lax.rem(c, 2)
    y = c // 2
    cx = y * 2 + (1 - x)
    cy = (1 - y) * 2 + x
    xpeer = (z * PLANE + cx, t)
    ypeer = (z * PLANE + cy, t)
    diagonal = (z * PLANE + PLANE - 1 - c, t)
    other = (d, 1 - t)
    top = planes - 1

    def at_plane(plane):
        return (plane * PLANE + c, t)

    tiles = cols // LANES
    na = max(1, (tiles * 2 + 10) // 19)
    nb = (tiles - 2 * na + 1) // 2
    ga = (0, na * LANES)
    gd = (na * LANES, na * LANES)
    gad = (0, 2 * na * LANES)
    gb = (2 * na * LANES, nb * LANES)
    gc = ((2 * na + nb) * LANES, cols - (2 * na + nb) * LANES)
    gbc = (2 * na * LANES, cols - 2 * na * LANES)

    def g(slot, count, group):
        start = slot * rows
        return gbuf.at[pl.ds(pl.multiple_of(start, rows), rows * count), pl.ds(*group)]

    def remote(ref, dst, send, recv, peer):
        return pltpu.make_async_remote_copy(
            src_ref=ref, dst_ref=dst, send_sem=send, recv_sem=recv,
            device_id=peer, device_id_type=pl.DeviceIdType.MESH,
        )

    loads = [
        pltpu.make_async_copy(grads_ref, g(d, 1, (0, cols)), lsem.at[0]),
        pltpu.make_async_copy(
            acts_ref, xplane.at[pl.ds(pl.multiple_of(c * rows, rows), rows), :], lsem.at[1]
        ),
    ]
    for load in loads:
        load.start()
    barrier = pltpu.get_barrier_semaphore()

    def greet(peer):
        pl.semaphore_signal(barrier, inc=1, device_id=peer, device_id_type=pl.DeviceIdType.MESH)

    others = [at_plane(lax.rem(z + step, planes)) for step in range(1, planes)]
    for peer in (xpeer, ypeer, diagonal, other, *others):
        greet(peer)
    pl.semaphore_wait(barrier, 3 + planes)
    for load in loads:
        load.wait()

    def line(plane, up):
        peer = at_plane(jnp.minimum(z + 1, top) if up else jnp.maximum(z - 1, 0))
        ref = g(plane * PLANE + c, 1, gbc)
        return remote(ref, ref, s_line.at[int(up), plane], r_line.at[plane], peer)

    def aline(plane, up):
        peer = at_plane(jnp.minimum(z + 1, top) if up else jnp.maximum(z - 1, 0))
        ref = g(plane * PLANE, PLANE, gad)
        return remote(ref, ref, s_aline.at[int(up), plane], r_aline.at[plane], peer)

    def pair(kind, plane):
        slot, group, peer = {
            0: (c, gb, ypeer),
            1: (c, gc, xpeer),
            2: (c, gb, xpeer),
            3: (cy, gb, xpeer),
            4: (c, gc, ypeer),
            5: (cx, gc, ypeer),
        }[kind]
        ref = g(plane * PLANE + slot, 1, group)
        return remote(ref, ref, s_pair.at[kind, plane], r_pair.at[kind, plane], peer)

    def one(kind):
        slot, count, group, peer = {
            0: (c, 1, ga, xpeer),
            1: (c, 1, gd, ypeer),
            2: (y * 2, 2, ga, ypeer),
            3: (c, 1, gd, xpeer),
            4: (cy, 1, gd, xpeer),
        }[kind]
        ref = g(z * PLANE + slot, count, group)
        return remote(ref, ref, s_one.at[kind], r_one.at[kind], peer)

    def xrows(slot, part=None):
        if part is None:
            return xplane.at[pl.ds(pl.multiple_of(slot * rows, rows), rows), :]
        size = rows // 2
        return xplane.at[pl.ds(pl.multiple_of(slot * rows + part * size, size), size), :]

    def xcopy(kind):
        ref, dst, peer = {
            0: (xrows(c), xrows(c), xpeer),
            1: (xrows(c), xrows(c), ypeer),
            2: (xrows(cx, 0), xrows(cx, 0), ypeer),
            3: (xrows(cy, 1), xrows(cy, 1), xpeer),
            4: (xrows(c), xcross, at_plane(lax.rem(z + top, planes))),
        }[kind]
        return remote(ref, dst, s_x.at[kind], r_x.at[kind], peer)

    def in_line(plane, sign, action):
        ok = (plane >= 0) if sign < 0 else (plane <= top)

        @pl.when(ok)
        def _():
            action(plane)

    def both(step, action):
        in_line(z - 1 - step, -1, functools.partial(action, up=True))
        in_line(z + 1 + step, 1, functools.partial(action, up=False))

    def forward(make, plane, up):
        @pl.when((z < top) if up else (z > 0))
        def _():
            make(plane, up).start()

    def start_pairs(kinds, plane):
        for kind in kinds:
            pair(kind, plane).start()

    one(0).start()
    one(1).start()
    for up in (True, False):
        forward(line, z, up)
    pair(1, z).start()
    pair(0, z).start()
    one(0).wait_recv()
    one(2).start()
    one(1).wait_recv()
    one(3).start()
    one(4).start()
    xcopy(0).start()
    xcopy(1).start()
    start_pairs((2, 4), z)
    for kind in (2, 3, 4):
        one(kind).wait_recv()
    for up in (True, False):
        forward(aline, z, up)
    xcopy(4).start()
    pair(1, z).wait_recv()
    pair(5, z).start()
    pair(0, z).wait_recv()
    pair(3, z).start()

    def line_arrived(plane, up):
        line(plane, up).wait_recv()
        forward(line, plane, up)
        start_pairs((0, 1, 2, 4), plane)

    def aline_arrived(plane, up):
        aline(plane, up).wait_recv()
        forward(aline, plane, up)

    def second(plane, up):
        pair(1, plane).wait_recv()
        pair(5, plane).start()
        pair(0, plane).wait_recv()
        pair(3, plane).start()

    both(0, line_arrived)
    xcopy(0).wait_recv()
    xcopy(2).start()
    xcopy(1).wait_recv()
    xcopy(3).start()
    both(0, aline_arrived)
    xcopy(2).wait_recv()
    xcopy(3).wait_recv()

    feats = xall.shape[1]
    per = half // (PLANE * feats)
    holder = z // per

    def share(plane):
        offset = (plane - t * per) * PLANE * feats + c * feats
        src = xplane.at[:, pl.ds(pl.multiple_of(offset, feats), feats)]
        dst = xall.at[pl.ds(pl.multiple_of(z * PLANE * rows, rows), PLANE * rows), :]
        return src, dst

    def a2a(plane, source):
        src, dst = share(plane)
        return remote(src, dst, s_a2a.at[plane], r_a2a.at[source], at_plane(plane))

    def local_share():
        src, dst = share(z)
        return pltpu.make_async_copy(src, dst, lsem.at[2])

    xcopy(4).wait_recv()
    dims = (((1,), (1,)), ((), ()))
    own_x = xplane[pl.ds(pl.multiple_of(c * rows, rows), rows), :]
    apart[:rows, :] = lax.dot_general(own_x, xplane[...], dims, preferred_element_type=jnp.float32)
    apart[rows:, :] = lax.dot_general(
        xcross[...], xplane[...], dims, preferred_element_type=jnp.float32
    )

    both(0, second)
    both(1, line_arrived)
    for plane in range(planes):
        @pl.when((plane // per == t) & (plane != z))
        def _(plane=plane):
            a2a(plane, z).start()

    @pl.when(holder == t)
    def _():
        local_share().start()

    both(1, aline_arrived)
    exchange = remote(apart, apeer, s_one.at[5], r_one.at[5], other)
    exchange.start()
    both(1, second)
    both(2, line_arrived)

    whole = remote(xall, xall, s_one.at[6], r_one.at[6], other)

    @pl.when(holder == t)
    def _():
        for step in range(1, planes):
            a2a(z, lax.rem(z + step, planes)).wait_recv()
        local_share().wait()
        whole.start()

    @pl.when(holder != t)
    def _():
        whole.wait_recv()

    both(2, second)

    exchange.wait()
    apart[...] = apart[...] + apeer[...]
    row = lax.broadcasted_iota(jnp.int32, (n, LANES), 0)
    lane = lax.broadcasted_iota(jnp.int32, (n, LANES), 1)
    coefs = jnp.zeros((n, LANES), jnp.float32)
    for slot in range(slots):
        coefs = coefs + jnp.where(
            lane == lax.rem(row + slot, n), coding_ref[:, slot : slot + 1].astype(jnp.float32), 0.0
        )

    for p in range(n):
        turned = jnp.transpose(xall[p * rows : (p + 1) * rows, :].astype(jnp.float32))
        lhs[:feats, p * rows : (p + 1) * rows] = turned.astype(jnp.bfloat16)

    both(2, aline_arrived)
    for plane in range(planes):
        for kind in (2, 3, 4, 5):
            pair(kind, plane).wait_recv()

    def products(slot, base):
        block = gbuf[pl.ds(pl.multiple_of(slot * rows, rows), rows), :]
        plane_rows = gbuf[pl.ds(pl.multiple_of(z * PLANE * rows, rows), PLANE * rows), :]
        grams = lax.dot_general(block, plane_rows, dims, preferred_element_type=jnp.float32)
        sums = jnp.sum(grams * apart[base : base + rows, :], axis=0, keepdims=True)
        return [
            jnp.sum(sums[:, k * rows : (k + 1) * rows], axis=1, keepdims=True) for k in range(PLANE)
        ]

    ahead = lax.rem(z + 1, planes) * PLANE + c
    total = jnp.zeros((n, LANES), jnp.float32)
    for k, value in enumerate(products(d, 0)):
        total = total + jnp.where((row == z * PLANE + k) & (lane == d), value, 0.0)
    for k, value in enumerate(products(ahead, rows)):
        p = z * PLANE + k
        here = ((row == p) & (lane == ahead)) | ((row == ahead) & (lane == p))
        total = total + jnp.where(here, value, 0.0)
    stages = ((other,), (diagonal, xpeer, ypeer), tuple(others))
    first = 0
    for stage, peers in enumerate(stages):
        msend[stage] = total
        hops = [
            remote(msend.at[stage], mrecv.at[first + k], s_m.at[first + k], r_m.at[first + k], peer)
            for k, peer in enumerate(peers)
        ]
        for hop in hops:
            hop.start()
        for hop in hops:
            hop.wait()
        for k in range(len(peers)):
            total = total + mrecv[first + k]
        first += len(peers)

    spread = jnp.zeros((n, LANES), jnp.float32)
    for p in range(n):
        spread = spread + coefs[:, p : p + 1] * total[p : p + 1, :]
    squares = jnp.sum(spread * coefs, axis=1, keepdims=True)
    factor = jnp.minimum(1.0, limit / jnp.sqrt(squares / entries + 1e-06))
    scaled = alive_ref[...].astype(jnp.float32) * factor * overall
    weights = jnp.sum(scaled * coefs, axis=0, keepdims=True)

    for p in range(n):
        block = lhs[:feats, p * rows : (p + 1) * rows].astype(jnp.float32)
        block = block * weights[:, p : p + 1]
        high = block.astype(jnp.bfloat16)
        lhs[:feats, p * rows : (p + 1) * rows] = high
        lhs[feats:, p * rows : (p + 1) * rows] = (block - high.astype(jnp.float32)).astype(
            jnp.bfloat16
        )

    def write(start, size):
        both_parts = jnp.dot(
            lhs[...], gbuf[:, pl.ds(start, size)], preferred_element_type=jnp.float32
        )
        out_ref[:, pl.ds(start, size)] = both_parts[:feats] + both_parts[feats:]

    wide = 2 * LANES

    @pl.loop(0, cols // wide)
    def _(tile):
        write(pl.multiple_of(tile * wide, wide), wide)

    if cols % wide:
        write(cols - cols % wide, cols % wide)

    for kind in range(5):
        one(kind).wait_send()
        xcopy(kind).wait_send()
    for plane in range(planes):
        for kind in range(6):
            pair(kind, plane).wait_send()

        @pl.when((plane // per == t) & (plane != z))
        def _(plane=plane):
            a2a(plane, z).wait_send()

        @pl.when((plane <= z) & (z < top))
        def _(plane=plane):
            line(plane, True).wait_send()
            aline(plane, True).wait_send()

        @pl.when((plane >= z) & (z > 0))
        def _(plane=plane):
            line(plane, False).wait_send()
            aline(plane, False).wait_send()

    @pl.when(holder == t)
    def _():
        whole.wait_send()


def gathered(activations, dgrad, coding, alive):
    workers = lax.axis_size("dp")
    rows, half = activations.shape
    cols = dgrad.shape[1]
    tensor = lax.axis_size("tensor")
    planes = workers // PLANE
    feats = half * tensor // workers
    limit = 8.0 * math.sqrt(rows)
    overall = 1.0 / (limit * math.sqrt(workers))
    body = functools.partial(
        kernel, planes, coding.shape[1], limit, overall, float(half * tensor * cols * tensor)
    )
    dma = pltpu.SemaphoreType.DMA
    vmem = pl.BlockSpec(memory_space=pltpu.VMEM)
    return pl.pallas_call(
        body,
        out_shape=jax.ShapeDtypeStruct((feats, cols), jnp.float32),
        in_specs=[pl.BlockSpec(memory_space=pl.ANY)] * 2 + [vmem] * 2,
        out_specs=vmem,
        scratch_shapes=[
            pltpu.VMEM((workers * rows, cols), jnp.bfloat16),
            pltpu.VMEM((PLANE * rows, half), jnp.bfloat16),
            pltpu.VMEM((rows, half), jnp.bfloat16),
            pltpu.VMEM((workers * rows, feats), jnp.bfloat16),
            pltpu.VMEM((2 * rows, PLANE * rows), jnp.float32),
            pltpu.VMEM((2 * rows, PLANE * rows), jnp.float32),
            pltpu.VMEM((3, workers, LANES), jnp.float32),
            pltpu.VMEM((3 + planes, workers, LANES), jnp.float32),
            pltpu.VMEM((2 * feats, workers * rows), jnp.bfloat16),
            dma((3,)),
            dma((2, planes)),
            dma((planes,)),
            dma((2, planes)),
            dma((planes,)),
            dma((6, planes)),
            dma((6, planes)),
            dma((7,)),
            dma((7,)),
            dma((5,)),
            dma((5,)),
            dma((planes,)),
            dma((planes,)),
            dma((3 + planes,)),
            dma((3 + planes,)),
        ],
        compiler_params=pltpu.CompilerParams(
            collective_id=0, has_side_effects=True, vmem_limit_bytes=VMEM_BUDGET
        ),
    )(activations, dgrad, coding, alive.reshape(workers, 1))


def fits(activations, dgrad, coding):
    workers = lax.axis_size("dp")
    rows, half = activations.shape
    cols = dgrad.shape[1]
    tensor = lax.axis_size("tensor")
    width = half * tensor
    planes = workers // PLANE
    return (
        tensor == 2
        and workers % PLANE == 0
        and PLANE <= workers <= LANES
        and planes >= 3
        and planes % tensor == 0
        and coding.shape[1] <= PLANE
        and rows == LANES
        and width == workers * LANES
        and cols % LANES == 0
        and cols >= 8 * LANES
        and workers * rows * cols * 2 <= VMEM_BUDGET // 2
    )


def step(activations, dgrad, coding, alive):
    if fits(activations, dgrad, coding):
        return gathered(activations, dgrad, coding, alive)
    return local(activations, dgrad, coding, alive)


def solution(mesh):
    return jax.shard_map(
        step,
        mesh=mesh,
        in_specs=(P("dp", "tensor"), P("dp", "tensor"), P(), P()),
        out_specs=P("dp", "tensor"),
        check_vma=False,
    )
```
